32 devices in a mesh: seq: 8 (over y, x, core), fsdp: 4 (over z).
Axes of the slice: x: 2, y: 2, z: 4, core: 2. Of those that a mesh axis runs over, the one named last changes fastest.
Arguments:
- tokens: bfloat16 [4096, 1024], P(('seq', 'fsdp')), may hold values from -6 to 6
- first_gain: float32 [1024], P(('seq', 'fsdp')), may hold values from 0.5 to 1.5
- first_bias: float32 [1024], P(('seq', 'fsdp')), may hold values from -0.5 to 0.5
- w_qkv: float32 [1024, 3072], P(('seq', 'fsdp')), may hold values from -0.1875 to 0.1875
- query_bias: float32 [1024], P(('seq', 'fsdp')), may hold values from -0.5 to 0.5
- value_bias: float32 [1024], P(('seq', 'fsdp')), may hold values from -0.5 to 0.5
- w_proj: float32 [1024, 1024], P(('seq', 'fsdp')), may hold values from -0.75 to 0.75
- proj_bias: float32 [1024], P(('seq', 'fsdp')), may hold values from -0.5 to 0.5
- second_gain: float32 [1024], P(('seq', 'fsdp')), may hold values from 0.5 to 1.5
- second_bias: float32 [1024], P(('seq', 'fsdp')), may hold values from -0.5 to 0.5
- w_up: float32 [1024, 4096], P(('seq', 'fsdp')), may hold values from -0.1875 to 0.1875
- up_bias: float32 [4096], P(('seq', 'fsdp')), may hold values from -0.5 to 0.5
- w_down: float32 [4096, 1024], P(('seq', 'fsdp')), may hold values from -0.09375 to 0.09375
- down_bias: float32 [1024], P(('seq', 'fsdp')), may hold values from -0.5 to 0.5
- cotangent: bfloat16 [4096, 1024], P(('seq', 'fsdp')), may hold values from -6 to 6
- seq_ids: int32 [4096], P(('seq', 'fsdp')), may hold values from 0 to 31, as said below
- offsets: int32 [4096], P(('seq', 'fsdp')), may hold values from 0 to 511, as said below
Outputs:
- output: bfloat16 [4096, 1024], P(('seq', 'fsdp'))
- grad_tokens: bfloat16 [4096, 1024], P(('seq', 'fsdp'))
- grad_first_gain: float32 [1024], P(('seq', 'fsdp'))
- grad_first_bias: float32 [1024], P(('seq', 'fsdp'))
- grad_w_qkv: float32 [1024, 3072], P(('seq', 'fsdp'))
- grad_query_bias: float32 [1024], P(('seq', 'fsdp'))
- grad_value_bias: float32 [1024], P(('seq', 'fsdp'))
- grad_w_proj: float32 [1024, 1024], P(('seq', 'fsdp'))
- grad_proj_bias: float32 [1024], P(('seq', 'fsdp'))
- grad_second_gain: float32 [1024], P(('seq', 'fsdp'))
- grad_second_bias: float32 [1024], P(('seq', 'fsdp'))
- grad_w_up: float32 [1024, 4096], P(('seq', 'fsdp'))
- grad_up_bias: float32 [4096], P(('seq', 'fsdp'))
- grad_w_down: float32 [4096, 1024], P(('seq', 'fsdp'))
- grad_down_bias: float32 [1024], P(('seq', 'fsdp'))
The draws below stay inside these ranges and needn't reach their ends.
Inputs may be any that keep to these rules, and one draw needn't show every extreme that they name: `seq_ids`: rows come in aligned blocks of 512 rows, each held by one group of fsdp devices; no sequence crosses a block. Half of the blocks, rounded up, hold one sequence of 512 rows; the others hold four sequences of 128 rows. Equal ids mark one sequence. `offsets`: the place of each row in its sequence, counting from 0.
All inputs are finite; a program needn't handle non-finite values.
Results may differ from the reference program's by a relative error of at most 0.012.
Values may be sent and summed in bfloat16 or wider, within the bound.
No kernel may reach another device: no remote copies, remote signals or barrier semaphores. Data moves between devices by JAX's collectives and lax.ppermute only.
A program may use at most 128 MiB of HBM per device.

```python
import math
import jax
import jax.numpy as jnp
from jax import lax

D = 1024
HEADS = 16
HDIM = 64
FF = 4096
GROUP = 512
TOKENS = 4096


def layout_rows(key):
    group_count = TOKENS // GROUP
    ranking = jax.random.permutation(jax.random.fold_in(key, 11), group_count)
    long_group = ranking < (group_count + 1) // 2
    row_index = jnp.arange(TOKENS, dtype=jnp.int32)
    group_index = row_index // GROUP
    within = row_index % GROUP
    short_len = GROUP // 4
    is_long = long_group[group_index]
    ids_out = jnp.where(is_long, 4 * group_index, 4 * group_index + within // short_len)
    places = jnp.where(is_long, within, within % short_len)
    return (ids_out.astype(jnp.int32), places.astype(jnp.int32))


def draw_seq_ids(key, part):
    return layout_rows(key)[0]


def draw_offsets(key, part):
    return layout_rows(key)[1]


def shard_levels(rng, dims, pieces, low, high):
    factor_of, own = 1.0, jax.random.fold_in(rng, 6)
    for axis_at, blocks in pieces:
        draws = jnp.exp(jax.random.uniform(jax.random.fold_in(own, axis_at), (blocks,), jnp.float32, low / len(pieces), high / len(pieces)))
        factor_of = factor_of * jnp.repeat(draws, dims[axis_at] // blocks).reshape([-1 if axis == axis_at else 1 for axis in range(len(dims))])
    return factor_of


def bell_draw(stream_key, extent, scale, most, shards=(), held_as=jnp.bfloat16):
    values = scale * jax.random.normal(stream_key, extent, jnp.float32)
    if shards:
        values = values * shard_levels(stream_key, extent, shards, -0.22, 0.18)
    return jnp.clip(values, -most, most).astype(held_as)


def setup_inputs(seed: int = 0) -> dict:
    key_list = jax.random.split(jax.random.key(seed), 18)
    return {
        "tokens": bell_draw(key_list[0], (TOKENS, D), 1.0, 6.0, ((0, 32),)),
        "first_gain": jnp.clip(1.0 + 0.1 * jax.random.normal(key_list[1], (D,), jnp.float32), 0.5, 1.5),
        "first_bias": jnp.clip(jax.random.uniform(key_list[2], (D,), jnp.float32, -0.5, 0.5) * shard_levels(key_list[2], (D,), ((0, 32),), -0.4, 0.0), -0.5, 0.5),
        "w_qkv": bell_draw(key_list[3], (D, 3 * D), D ** -0.5, 0.1875, ((0, 32),), jnp.float32),
        "query_bias": jnp.clip(jax.random.uniform(key_list[4], (D,), jnp.float32, -0.5, 0.5) * shard_levels(key_list[4], (D,), ((0, 32),), -0.4, 0.0), -0.5, 0.5),
        "value_bias": jnp.clip(jax.random.uniform(key_list[5], (D,), jnp.float32, -0.5, 0.5) * shard_levels(key_list[5], (D,), ((0, 32),), -0.4, 0.0), -0.5, 0.5),
        "w_proj": bell_draw(key_list[6], (D, D), (D // 16) ** -0.5, 0.75, ((0, 32),), jnp.float32),
        "proj_bias": jnp.clip(jax.random.uniform(key_list[7], (D,), jnp.float32, -0.5, 0.5) * shard_levels(key_list[7], (D,), ((0, 32),), -0.4, 0.0), -0.5, 0.5),
        "second_gain": jnp.clip(1.0 + 0.1 * jax.random.normal(key_list[8], (D,), jnp.float32), 0.5, 1.5),
        "second_bias": jnp.clip(jax.random.uniform(key_list[9], (D,), jnp.float32, -0.5, 0.5) * shard_levels(key_list[9], (D,), ((0, 32),), -0.4, 0.0), -0.5, 0.5),
        "w_up": bell_draw(key_list[10], (D, FF), D ** -0.5, 0.1875, ((0, 32),), jnp.float32),
        "up_bias": jnp.clip(jax.random.uniform(key_list[11], (FF,), jnp.float32, -0.5, 0.5) * shard_levels(key_list[11], (FF,), ((0, 32),), -0.4, 0.0), -0.5, 0.5),
        "w_down": bell_draw(key_list[12], (FF, D), FF ** -0.5, 0.09375, ((0, 32),), jnp.float32),
        "down_bias": jnp.clip(jax.random.uniform(key_list[13], (D,), jnp.float32, -0.5, 0.5) * shard_levels(key_list[13], (D,), ((0, 32),), -0.4, 0.0), -0.5, 0.5),
        "cotangent": bell_draw(key_list[14], (TOKENS, D), 1.0, 6.0, ((0, 32),)),
        "seq_ids": draw_seq_ids(jax.random.fold_in(key_list[17], 71), 0),
        "offsets": draw_offsets(jax.random.fold_in(key_list[17], 71), 0),
    }


@jax.custom_vjp
def low(v):
    return lax.optimization_barrier(v.astype(jnp.bfloat16)).astype(jnp.float32)

@jax.custom_vjp
def low_back(v):
    return v

def low_keep(v):
    return (low(v), None)

def low_pass(kept, grad):
    return (grad,)

def back_keep(v):
    return (v, None)

def back_low(kept, grad):
    return (low(grad),)
low.defvjp(low_keep, low_pass)
low_back.defvjp(back_keep, back_low)
EPSILON = 1e-05

def rounded(values):
    return low_back(low(values))

def layer_norm(values, gain, bias):
    centred = values - lax.optimization_barrier(jnp.mean(values, axis=-1, keepdims=True))
    spread = lax.optimization_barrier(jnp.mean(centred * centred, axis=-1, keepdims=True))
    return centred * lax.rsqrt(spread + EPSILON) * gain + bias

def matmul(left, right):
    return jnp.dot(left, right, preferred_element_type=jnp.float32, precision=lax.Precision.HIGHEST)

def attend_group(inputs):
    queries, all_keys, all_values, group_ids, group_places = inputs
    scores = jnp.einsum('qhd,khd->hqk', queries, all_keys, precision=lax.Precision.HIGHEST) * (1.0 / math.sqrt(HDIM))
    scores = low_back(scores)
    visible = (group_ids[:, None] == group_ids[None, :]) & (group_places[None, :] <= group_places[:, None])
    scores = jnp.where(visible[None], scores, jnp.float32(-1e+30))
    row_max = lax.optimization_barrier(jnp.max(scores, axis=-1, keepdims=True))
    shifted = jnp.exp(scores - row_max)
    softmax_w = shifted / lax.optimization_barrier(jnp.sum(shifted, axis=-1, keepdims=True))
    return jnp.einsum('hqk,khd->qhd', low(softmax_w), all_values, precision=lax.Precision.HIGHEST)

def layer(params, seq_ids, offsets):
    tokens, first_gain, first_bias, w_qkv, query_bias, value_bias, w_proj, proj_bias, second_gain, second_bias, w_up, up_bias, w_down, down_bias = params
    model_width = tokens.shape[1]
    row_total = tokens.shape[0]
    group_count = row_total // GROUP
    normed = low(layer_norm(tokens, first_gain, first_bias))
    joined = matmul(normed, low(w_qkv))
    queries = rounded(joined[:, :model_width] + query_bias)
    key_rows = rounded(joined[:, model_width:2 * model_width])
    value_rows = rounded(joined[:, 2 * model_width:] + value_bias)

    def shaped(matrix):
        return matrix.reshape(group_count, GROUP, HEADS, HDIM)
    mixed_heads = lax.map(jax.checkpoint(attend_group), (shaped(queries), shaped(key_rows), shaped(value_rows), seq_ids.reshape(group_count, GROUP), offsets.reshape(group_count, GROUP)))
    mixed_heads = rounded(mixed_heads.reshape(row_total, model_width))
    attended = low_back(matmul(mixed_heads, low(w_proj)) + proj_bias)
    middle = tokens + attended
    second_normed = low(layer_norm(middle, second_gain, second_bias))
    preact = low_back(matmul(second_normed, low(w_up)) + up_bias)
    activated = low(jax.nn.gelu(preact, approximate=True))
    return middle + low_back(matmul(activated, low(w_down)) + down_bias)

def reference(tokens, first_gain, first_bias, w_qkv, query_bias, value_bias, w_proj, proj_bias, second_gain, second_bias, w_up, up_bias, w_down, down_bias, cotangent, seq_ids, offsets):
    params = (tokens.astype(jnp.float32), first_gain, first_bias, w_qkv, query_bias, value_bias, w_proj, proj_bias, second_gain, second_bias, w_up, up_bias, w_down, down_bias)

    def closed(inputs):
        return layer(inputs, seq_ids, offsets)
    result, pull_back = jax.vjp(closed, params)
    grads = pull_back(cotangent.astype(jnp.float32))[0]
    return (result.astype(jnp.bfloat16), grads[0].astype(jnp.bfloat16), grads[1], grads[2], grads[3], grads[4], grads[5], grads[6], grads[7], grads[8], grads[9], grads[10], grads[11], grads[12], grads[13])
```

```python
import math

import jax
import jax.numpy as jnp
from jax import lax
from jax.sharding import PartitionSpec as P

HDIM = 64
EPSILON = 1e-05
BF = jnp.bfloat16
F32 = jnp.float32


def mm(left, right):
    return jnp.dot(left, right, preferred_element_type=F32)


def mm_t(left, right):
    return lax.dot_general(left, right, (((1,), (1,)), ((), ())), preferred_element_type=F32)


def t_mm(left, right):
    return lax.dot_general(left, right, (((0,), (0,)), ((), ())), preferred_element_type=F32)


def norm_parts(values):
    centred = values - jnp.mean(values, axis=-1, keepdims=True)
    spread = jnp.mean(centred * centred, axis=-1, keepdims=True)
    scale = lax.rsqrt(spread + EPSILON)
    return centred * scale, scale


def norm_back(grad, gain, xhat, scale):
    gh = grad * gain
    return (
        gh - jnp.mean(gh, axis=-1, keepdims=True) - xhat * jnp.mean(gh * xhat, axis=-1, keepdims=True)
    ) * scale


def gelu(values):
    return jax.nn.gelu(values, approximate=True)


class Net:
    def __init__(self, seq, fsdp):
        self.S, self.F = seq, fsdp
        self.s = lax.axis_index("seq")
        self.f = lax.axis_index("fsdp")
        bits = [1 << i for i in range(seq.bit_length() - 1)]
        if seq == 8:
            self.orders = ([1, 2, 4], [1, 4, 2])
        else:
            self.orders = (bits,)

    def shift(self, x, k):
        return lax.ppermute(x, "fsdp", [(i, (i + k) % self.F) for i in range(self.F)])

    def swap(self, x, bit):
        return lax.ppermute(x, "seq", [(i, i ^ bit) for i in range(self.S)])

    def gather_rel(self, x):
        return [x] + [self.shift(x, k) for k in range(1, self.F)]

    def scatter_sum(self, parts):
        total = parts[0].astype(F32)
        for k in range(1, self.F):
            total = total + self.shift(parts[(self.F - k) % self.F], k).astype(F32)
        return total

    def to_absolute(self, pieces, axis):
        F = self.F
        line = jnp.concatenate([pieces[(F - 1 - i) % F] for i in range(2 * F - 1)], axis=axis)
        size = pieces[0].shape[axis]
        return lax.dynamic_slice_in_dim(line, (F - 1 - self.f) * size, F * size, axis=axis)

    def exchange_pieces(self, x):
        F = self.F
        pick = lambda k: lax.dynamic_index_in_dim(x, (self.f + k) % F, 0, keepdims=False)
        return [pick(0)] + [self.shift(pick(k), k) for k in range(1, F)]

    def gather_seq(self, x):
        parts = len(self.orders)
        c, n = x.shape
        outs = []
        for p, order in enumerate(self.orders):
            h = c // parts
            cur = x[p * h : (p + 1) * h].reshape(1, h, n)
            have = []
            for bit in reversed(order):
                got = self.swap(cur, bit)
                low = 1
                for b in have:
                    if b < bit:
                        low *= 2
                high = cur.shape[0] // low
                a = cur.reshape(high, 1, low, h, n)
                b_ = got.reshape(high, 1, low, h, n)
                mine = (self.s & bit) != 0
                cur = jnp.where(
                    mine, jnp.concatenate([b_, a], axis=1), jnp.concatenate([a, b_], axis=1)
                ).reshape(high * 2 * low, h, n)
                have.append(bit)
            outs.append(cur)
        out = outs[0] if parts == 1 else jnp.concatenate(outs, axis=1)
        return out.reshape(self.S * c, n)

    def scatter_seq(self, x, dtype):
        parts = len(self.orders)
        S, c, n = x.shape
        outs = []
        for p, order in enumerate(self.orders):
            h = c // parts
            cur = x[:, p * h : (p + 1) * h]
            left = sorted(order)
            for at, bit in enumerate(order):
                low = 1
                for b in left:
                    if b < bit:
                        low *= 2
                high = cur.shape[0] // (2 * low)
                view = cur.reshape(high, 2, low, h, n)
                my = jnp.where((self.s & bit) != 0, 1, 0)
                keep = lax.dynamic_index_in_dim(view, my, 1, keepdims=False)
                give = lax.dynamic_index_in_dim(view, 1 - my, 1, keepdims=False)
                got = self.swap(give.astype(dtype), bit)
                cur = (keep.astype(F32) + got.astype(F32)).reshape(high * low, h, n)
                if at + 1 < len(order):
                    cur = cur.astype(dtype)
                left.remove(bit)
            outs.append(cur.reshape(h, n))
        return outs[0] if parts == 1 else jnp.concatenate(outs, axis=0)


def on_device(sizes, *args):
    (
        tokens,
        first_gain,
        first_bias,
        w_qkv,
        query_bias,
        value_bias,
        w_proj,
        proj_bias,
        second_gain,
        second_bias,
        w_up,
        up_bias,
        w_down,
        down_bias,
        cotangent,
        seq_ids,
        offsets,
    ) = args
    S, F = sizes
    net = Net(S, F)
    f = net.f
    rows, width = tokens.shape
    wr = w_qkv.shape[0]
    ff = w_up.shape[1]
    ur = w_down.shape[0]
    lw = width // F
    lh = lw // HDIM
    lu = ff // F
    group = rows * F

    vec = jnp.concatenate(
        [first_gain, first_bias, query_bias, value_bias, proj_bias, second_gain, second_bias, down_bias, up_bias]
    )
    nv = vec.shape[0]
    high = lax.reduce_precision(vec, 8, 7)
    small = jnp.concatenate([high, vec - high]).astype(BF).reshape(wr, -1)
    vc = small.shape[1]
    rest = jnp.stack([seq_ids, offsets // 256, offsets % 256]).astype(BF).reshape(wr, -1)
    rc = rest.shape[1]
    pad = -(vc + rc) % 128
    small = jnp.concatenate([small, rest, jnp.zeros((wr, pad), BF)], axis=1)
    sc = vc + rc + pad
    qkv = w_qkv.astype(BF).reshape(wr, 3, F, lw).transpose(2, 0, 1, 3).reshape(F, wr, 3 * lw)
    up = w_up.astype(BF).reshape(wr, S, F, ur).transpose(2, 0, 1, 3).reshape(F, wr, lu)
    same = jnp.broadcast_to(small[None], (F, wr, sc))
    proj = jnp.broadcast_to(w_proj.astype(BF)[None], (F, wr, width))
    message = jnp.concatenate([qkv, same, up, proj], axis=2)
    pieces = net.exchange_pieces(message)
    held = net.to_absolute(pieces, 0)
    qc = 3 * lw + sc
    first = net.gather_seq(held[:, :qc])
    later = net.gather_seq(jnp.concatenate([held[:, qc:], w_down.astype(BF)], axis=1))
    qkv = first[:, : 3 * lw]
    up, proj, down = later[:, :lu], later[:, lu : lu + width], later[:, lu + width :]
    vec_all = first[:, 3 * lw : 3 * lw + vc].reshape(S, F, 2 * nv).astype(F32)
    vec_all = vec_all[:, :, :nv] + vec_all[:, :, nv:]
    places = [p[:, 3 * lw + vc : 3 * lw + vc + rc].reshape(3, rows) for p in pieces]
    tokens_later, _ = lax.optimization_barrier((tokens, pieces))
    blocks = net.gather_rel(tokens_later)
    cot_later, _ = lax.optimization_barrier((cotangent, blocks))
    cots = net.gather_rel(cot_later)

    def vector(i):
        return vec_all[:, :, i * wr : (i + 1) * wr].reshape(width)

    g1, b1, qb, vb, pb, g2, b2, db = [vector(i) for i in range(8)]
    ub = lax.dynamic_index_in_dim(vec_all[:, :, 8 * wr :], f, 1, keepdims=False).reshape(lu)
    qb = lax.dynamic_slice_in_dim(qb, f * lw, lw)
    vb = lax.dynamic_slice_in_dim(vb, f * lw, lw)

    tok = jnp.concatenate(blocks, axis=0).astype(F32)
    place = jnp.concatenate(places, axis=1).astype(jnp.int32)
    ids, offs = place[0], place[1] * 256 + place[2]
    visible = (ids[:, None] == ids[None, :]) & (offs[None, :] <= offs[:, None])
    xhat1, scale1 = norm_parts(tok)
    normed = (xhat1 * g1 + b1).astype(BF)
    joined = mm(normed, qkv)
    queries = (joined[:, :lw] + qb).astype(BF).reshape(group, lh, HDIM)
    keys = joined[:, lw : 2 * lw].astype(BF).reshape(group, lh, HDIM)
    values = (joined[:, 2 * lw :] + vb).astype(BF).reshape(group, lh, HDIM)
    score_scale = 1.0 / math.sqrt(HDIM)
    scores = jnp.einsum("qhd,khd->hqk", queries, keys, preferred_element_type=F32) * score_scale
    scores = jnp.where(visible[None], scores, F32(-1e30))
    shifted = jnp.exp(scores - jnp.max(scores, axis=-1, keepdims=True))
    probs = shifted / jnp.sum(shifted, axis=-1, keepdims=True)
    probs_low = probs.astype(BF)
    mixed = jnp.einsum("hqk,khd->qhd", probs_low, values, preferred_element_type=F32)
    mixed = mixed.reshape(group, lw).astype(BF)
    mixed_all = [jnp.roll(m, k * rows, axis=0) for k, m in enumerate(net.gather_rel(mixed))]
    mixed_all = net.to_absolute(mixed_all, 1)

    middle = tok + mm(mixed_all, proj) + pb
    xhat2, scale2 = norm_parts(middle)
    second = (xhat2 * g2 + b2).astype(BF)
    preact = mm(second, up) + ub
    activated, gelu_back = jax.vjp(gelu, preact)
    activated = activated.astype(BF)
    result = mm(activated, down).astype(BF).reshape(F, rows, width)
    cot = jnp.concatenate(cots, axis=0)
    gw_down = t_mm(activated, cot).astype(BF).reshape(S, ur, width)
    grad_act = mm_t(cot, down)
    grad_preact = gelu_back(grad_act)[0].astype(BF)
    gw_up = t_mm(second, grad_preact).astype(BF).reshape(S, F * wr, lu)
    grad_ub = jnp.sum(grad_preact.astype(F32), axis=0)
    part2 = mm_t(grad_preact, up)
    grad_g2 = jnp.sum(part2 * xhat2, axis=0)
    grad_b2 = jnp.sum(part2, axis=0)
    part2 = part2.astype(BF).reshape(F, rows, width)
    grad_second = net.scatter_sum([part2[k] for k in range(F)])
    upstream = cotangent.astype(F32)
    grad_middle = upstream + norm_back(grad_second, g2, xhat2[:rows], scale2[:rows])
    att = grad_middle.astype(BF)
    atts = jnp.concatenate(net.gather_rel(att), axis=0)

    result, _ = lax.optimization_barrier((result, atts))
    result = net.scatter_sum([result[k] for k in range(F)])
    output = (middle[:rows] + result + db).astype(BF)

    proj_own = lax.dynamic_slice_in_dim(proj, f * lw, lw, axis=0)
    grad_mixed = mm_t(atts, proj_own).astype(BF).reshape(group, lh, HDIM)
    grad_probs = jnp.einsum("qhd,khd->hqk", grad_mixed, values, preferred_element_type=F32)
    delta = jnp.sum(grad_probs * probs, axis=-1, keepdims=True)
    grad_scores = (probs * (grad_probs - delta)).astype(BF)
    grad_q = jnp.einsum("hqk,khd->qhd", grad_scores, keys, preferred_element_type=F32) * score_scale
    grad_k = jnp.einsum("hqk,qhd->khd", grad_scores, queries, preferred_element_type=F32) * score_scale
    grad_v = jnp.einsum("hqk,qhd->khd", probs_low, grad_mixed, preferred_element_type=F32)
    grad_q, grad_k, grad_v = [g.reshape(group, lw).astype(BF) for g in (grad_q, grad_k, grad_v)]
    grad_joined = jnp.concatenate([grad_q, grad_k, grad_v], axis=1)
    gw_proj = t_mm(mixed_all, atts).astype(BF).reshape(S, F, wr, width)
    gw_proj = lax.dynamic_index_in_dim(gw_proj, f, 1, keepdims=False)
    gw_qkv = t_mm(normed, grad_joined).astype(BF).reshape(S, F * wr, 3 * lw)
    part1 = mm_t(grad_joined, qkv)
    grad_g1 = jnp.sum(part1 * xhat1, axis=0)
    grad_b1 = jnp.sum(part1, axis=0)
    part1 = part1.astype(BF).reshape(F, rows, width)
    grad_first = net.scatter_sum([part1[k] for k in range(F)])
    grad_tokens = (grad_middle + norm_back(grad_first, g1, xhat1[:rows], scale1[:rows])).astype(BF)

    g_mlp = net.scatter_seq(jnp.concatenate([gw_down, gw_up], axis=2), BF)
    g_down = g_mlp[:, :width]
    g_up = g_mlp[:, width:].astype(BF).reshape(F, wr, lu)
    g_up = [p.reshape(wr, S, 1, ur) for p in net.exchange_pieces(g_up)]
    g_up = net.to_absolute(g_up, 2).astype(F32).reshape(wr, ff)
    gw_proj = gw_proj.reshape(S, wr, F, lw).transpose(0, 2, 1, 3).reshape(S, F * wr, lw)
    g_att = net.scatter_seq(jnp.concatenate([gw_qkv, gw_proj], axis=2), BF)
    g_proj = g_att[:, 3 * lw :].reshape(F, wr, lw).transpose(1, 0, 2).reshape(wr, width)
    g_qkv = g_att[:, : 3 * lw].astype(BF).reshape(F, wr, 3 * lw)
    g_qkv = [p.reshape(wr, 3, 1, lw) for p in net.exchange_pieces(g_qkv)]
    g_qkv = net.to_absolute(g_qkv, 2).astype(F32).reshape(wr, 3 * width)

    def spread(v):
        return lax.dynamic_update_slice_in_dim(jnp.zeros((width,), F32), v, f * lw, 0)

    full = [
        grad_g1,
        grad_b1,
        spread(jnp.sum(grad_q.astype(F32), axis=0)),
        spread(jnp.sum(grad_v.astype(F32), axis=0)),
        jnp.sum(att.astype(F32), axis=0),
        grad_g2,
        grad_b2,
        jnp.sum(upstream, axis=0),
    ]
    full = jnp.concatenate([v.reshape(S, F, wr) for v in full], axis=2)
    units = lax.dynamic_update_slice_in_dim(
        jnp.zeros((S, F, ur), F32), grad_ub.reshape(S, 1, ur), f, 1
    )
    sums = jnp.concatenate([full, units], axis=2)
    sums = scatter_small(net, sums)
    pick = lambda k: lax.dynamic_index_in_dim(sums, (f + k) % F, 0, keepdims=False)
    mine = pick(0)
    for k in range(1, F):
        mine = mine + net.shift(pick(k), k)
    v = [mine[i * wr : (i + 1) * wr] for i in range(8)]
    grad_up_bias = mine[8 * wr :]
    return (
        output,
        grad_tokens,
        v[0],
        v[1],
        g_qkv,
        v[2],
        v[3],
        g_proj,
        v[4],
        v[5],
        v[6],
        g_up,
        grad_up_bias,
        g_down,
        v[7],
    )


def scatter_small(net, x):
    cur = x
    bit = net.S // 2
    while bit:
        view = cur.reshape(2, bit, *x.shape[1:])
        my = jnp.where((net.s & bit) != 0, 1, 0)
        keep = lax.dynamic_index_in_dim(view, my, 0, keepdims=False)
        give = lax.dynamic_index_in_dim(view, 1 - my, 0, keepdims=False)
        cur = keep + net.swap(give, bit)
        bit //= 2
    return cur[0]


def solution(mesh):
    both = ("seq", "fsdp")
    mat, vec = P(both, None), P(both)
    sizes = (mesh.shape["seq"], mesh.shape["fsdp"])

    def body(*args):
        return on_device(sizes, *args)

    return jax.shard_map(
        body,
        mesh=mesh,
        in_specs=(mat, vec, vec, mat, vec, vec, mat, vec, vec, vec, mat, vec, mat, vec, mat, vec, vec),
        out_specs=(mat, mat, vec, vec, mat, vec, vec, mat, vec, vec, vec, mat, vec, mat, vec),
        check_vma=False,
    )
```

```python
import math

import jax
import jax.numpy as jnp
from jax import lax
from jax.sharding import PartitionSpec as P

HDIM = 64
EPSILON = 1e-05
BF = jnp.bfloat16
F32 = jnp.float32


def mm(left, right):
    return jnp.dot(left, right, preferred_element_type=F32)


def mm_t(left, right):
    return lax.dot_general(left, right, (((1,), (1,)), ((), ())), preferred_element_type=F32)


def t_mm(left, right):
    return lax.dot_general(left, right, (((0,), (0,)), ((), ())), preferred_element_type=F32)


def norm_parts(values):
    centred = values - jnp.mean(values, axis=-1, keepdims=True)
    spread = jnp.mean(centred * centred, axis=-1, keepdims=True)
    scale = lax.rsqrt(spread + EPSILON)
    return centred * scale, scale


def norm_back(grad, gain, xhat, scale):
    gh = grad * gain
    return (
        gh - jnp.mean(gh, axis=-1, keepdims=True) - xhat * jnp.mean(gh * xhat, axis=-1, keepdims=True)
    ) * scale


def gelu(values):
    return jax.nn.gelu(values, approximate=True)


class Net:
    def __init__(self, seq, fsdp):
        self.S, self.F = seq, fsdp
        self.s = lax.axis_index("seq")
        self.f = lax.axis_index("fsdp")
        bits = [1 << i for i in range(seq.bit_length() - 1)]
        if seq == 8:
            self.orders = ([1, 2, 4], [1, 4, 2])
        else:
            self.orders = (bits,)

    def shift(self, x, k):
        return lax.ppermute(x, "fsdp", [(i, (i + k) % self.F) for i in range(self.F)])

    def swap(self, x, bit):
        return lax.ppermute(x, "seq", [(i, i ^ bit) for i in range(self.S)])

    def gather_rel(self, x):
        return [x] + [self.shift(x, k) for k in range(1, self.F)]

    def scatter_sum(self, parts):
        total = parts[0].astype(F32)
        for k in range(1, self.F):
            total = total + self.shift(parts[(self.F - k) % self.F], k).astype(F32)
        return total

    def to_absolute(self, pieces, axis):
        F = self.F
        line = jnp.concatenate([pieces[(F - 1 - i) % F] for i in range(2 * F - 1)], axis=axis)
        size = pieces[0].shape[axis]
        return lax.dynamic_slice_in_dim(line, (F - 1 - self.f) * size, F * size, axis=axis)

    def exchange_pieces(self, x):
        F = self.F
        pick = lambda k: lax.dynamic_index_in_dim(x, (self.f + k) % F, 0, keepdims=False)
        return [pick(0)] + [self.shift(pick(k), k) for k in range(1, F)]

    def gather_seq(self, x):
        parts = len(self.orders)
        c, n = x.shape
        outs = []
        for p, order in enumerate(self.orders):
            h = c // parts
            cur = x[p * h : (p + 1) * h].reshape(1, h, n)
            have = []
            for bit in reversed(order):
                got = self.swap(cur, bit)
                low = 1
                for b in have:
                    if b < bit:
                        low *= 2
                high = cur.shape[0] // low
                a = cur.reshape(high, 1, low, h, n)
                b_ = got.reshape(high, 1, low, h, n)
                mine = (self.s & bit) != 0
                cur = jnp.where(
                    mine, jnp.concatenate([b_, a], axis=1), jnp.concatenate([a, b_], axis=1)
                ).reshape(high * 2 * low, h, n)
                have.append(bit)
            outs.append(cur)
        out = outs[0] if parts == 1 else jnp.concatenate(outs, axis=1)
        return out.reshape(self.S * c, n)

    def scatter_seq(self, x, dtype):
        parts = len(self.orders)
        S, c, n = x.shape
        outs = []
        for p, order in enumerate(self.orders):
            h = c // parts
            cur = x[:, p * h : (p + 1) * h]
            left = sorted(order)
            for at, bit in enumerate(order):
                low = 1
                for b in left:
                    if b < bit:
                        low *= 2
                high = cur.shape[0] // (2 * low)
                view = cur.reshape(high, 2, low, h, n)
                my = jnp.where((self.s & bit) != 0, 1, 0)
                keep = lax.dynamic_index_in_dim(view, my, 1, keepdims=False)
                give = lax.dynamic_index_in_dim(view, 1 - my, 1, keepdims=False)
                got = self.swap(give.astype(dtype), bit)
                cur = (keep.astype(F32) + got.astype(F32)).reshape(high * low, h, n)
                if at + 1 < len(order):
                    cur = cur.astype(dtype)
                left.remove(bit)
            outs.append(cur.reshape(h, n))
        return outs[0] if parts == 1 else jnp.concatenate(outs, axis=0)


def on_device(sizes, *args):
    (
        tokens,
        first_gain,
        first_bias,
        w_qkv,
        query_bias,
        value_bias,
        w_proj,
        proj_bias,
        second_gain,
        second_bias,
        w_up,
        up_bias,
        w_down,
        down_bias,
        cotangent,
        seq_ids,
        offsets,
    ) = args
    S, F = sizes
    net = Net(S, F)
    f = net.f
    rows, width = tokens.shape
    wr = w_qkv.shape[0]
    ff = w_up.shape[1]
    ur = w_down.shape[0]
    lw = width // F
    lh = lw // HDIM
    lu = ff // F
    group = rows * F

    vec = jnp.concatenate(
        [first_gain, first_bias, query_bias, value_bias, proj_bias, second_gain, second_bias, down_bias, up_bias]
    )
    nv = vec.shape[0]
    high = lax.optimization_barrier(vec.astype(BF))
    small = jnp.concatenate([high, (vec - high.astype(F32)).astype(BF)]).reshape(wr, -1)
    vc = small.shape[1]
    rest = jnp.stack([seq_ids, offsets // 256, offsets % 256]).astype(BF).reshape(wr, -1)
    rc = rest.shape[1]
    pad = -(vc + rc) % 128
    small = jnp.concatenate([small, rest, jnp.zeros((wr, pad), BF)], axis=1)
    sc = vc + rc + pad
    qkv = w_qkv.astype(BF).reshape(wr, 3, F, lw).transpose(2, 0, 1, 3).reshape(F, wr, 3 * lw)
    up = w_up.astype(BF).reshape(wr, S, F, ur).transpose(2, 0, 1, 3).reshape(F, wr, lu)
    same = jnp.broadcast_to(small[None], (F, wr, sc))
    pieces = net.exchange_pieces(jnp.concatenate([qkv, same], axis=2))
    first = net.gather_seq(net.to_absolute(pieces, 0))
    qkv = first[:, : 3 * lw]
    tokens_later, _ = lax.optimization_barrier((tokens, pieces))
    blocks = net.gather_rel(tokens_later)
    proj = jnp.broadcast_to(w_proj.astype(BF)[None], (F, wr, width))
    message, _ = lax.optimization_barrier((jnp.concatenate([up, proj], axis=2), blocks))
    later = net.exchange_pieces(message)
    cot_later, _ = lax.optimization_barrier((cotangent, later))
    cots = net.gather_rel(cot_later)
    later = jnp.concatenate([net.to_absolute(later, 0), w_down.astype(BF)], axis=1)
    later = net.gather_seq(later)
    up, proj, down = later[:, :lu], later[:, lu : lu + width], later[:, lu + width :]
    vec_all = first[:, 3 * lw : 3 * lw + vc].reshape(S, F, 2 * nv).astype(F32)
    vec_all = vec_all[:, :, :nv] + vec_all[:, :, nv:]
    places = [p[:, 3 * lw + vc : 3 * lw + vc + rc].reshape(3, rows) for p in pieces]

    def vector(i):
        return vec_all[:, :, i * wr : (i + 1) * wr].reshape(width)

    g1, b1, qb, vb, pb, g2, b2, db = [vector(i) for i in range(8)]
    ub = lax.dynamic_index_in_dim(vec_all[:, :, 8 * wr :], f, 1, keepdims=False).reshape(lu)
    qb = lax.dynamic_slice_in_dim(qb, f * lw, lw)
    vb = lax.dynamic_slice_in_dim(vb, f * lw, lw)

    tok = jnp.concatenate(blocks, axis=0).astype(F32)
    place = jnp.concatenate(places, axis=1).astype(jnp.int32)
    ids, offs = place[0], place[1] * 256 + place[2]
    visible = (ids[:, None] == ids[None, :]) & (offs[None, :] <= offs[:, None])
    xhat1, scale1 = norm_parts(tok)
    normed = (xhat1 * g1 + b1).astype(BF)
    joined = mm(normed, qkv)
    queries = (joined[:, :lw] + qb).astype(BF).reshape(group, lh, HDIM)
    keys = joined[:, lw : 2 * lw].astype(BF).reshape(group, lh, HDIM)
    values = (joined[:, 2 * lw :] + vb).astype(BF).reshape(group, lh, HDIM)
    score_scale = 1.0 / math.sqrt(HDIM)
    scores = jnp.einsum("qhd,khd->hqk", queries, keys, preferred_element_type=F32) * score_scale
    scores = jnp.where(visible[None], scores, F32(-1e30))
    shifted = jnp.exp(scores - jnp.max(scores, axis=-1, keepdims=True))
    probs = shifted / jnp.sum(shifted, axis=-1, keepdims=True)
    probs_low = probs.astype(BF)
    mixed = jnp.einsum("hqk,khd->qhd", probs_low, values, preferred_element_type=F32)
    mixed = mixed.reshape(group, lw).astype(BF)
    mixed_all = [jnp.roll(m, k * rows, axis=0) for k, m in enumerate(net.gather_rel(mixed))]
    mixed_all = net.to_absolute(mixed_all, 1)

    middle = tok + mm(mixed_all, proj) + pb
    xhat2, scale2 = norm_parts(middle)
    second = (xhat2 * g2 + b2).astype(BF)
    preact = mm(second, up) + ub
    activated, gelu_back = jax.vjp(gelu, preact)
    activated = activated.astype(BF)
    result = mm(activated, down).astype(BF).reshape(F, rows, width)
    cot = jnp.concatenate(cots, axis=0)
    gw_down = t_mm(activated, cot).astype(BF).reshape(S, ur, width)
    grad_act = mm_t(cot, down)
    grad_preact = gelu_back(grad_act)[0].astype(BF)
    gw_up = t_mm(second, grad_preact).astype(BF).reshape(S, F * wr, lu)
    grad_ub = jnp.sum(grad_preact.astype(F32), axis=0)
    part2 = mm_t(grad_preact, up)
    grad_g2 = jnp.sum(part2 * xhat2, axis=0)
    grad_b2 = jnp.sum(part2, axis=0)
    part2 = part2.astype(BF).reshape(F, rows, width)
    grad_second = net.scatter_sum([part2[k] for k in range(F)])
    upstream = cotangent.astype(F32)
    grad_middle = upstream + norm_back(grad_second, g2, xhat2[:rows], scale2[:rows])
    att = grad_middle.astype(BF)
    atts = jnp.concatenate(net.gather_rel(att), axis=0)

    result, _ = lax.optimization_barrier((result, atts))
    result = net.scatter_sum([result[k] for k in range(F)])
    output = (middle[:rows] + result + db).astype(BF)

    proj_own = lax.dynamic_slice_in_dim(proj, f * lw, lw, axis=0)
    grad_mixed = mm_t(atts, proj_own).astype(BF).reshape(group, lh, HDIM)
    grad_probs = jnp.einsum("qhd,khd->hqk", grad_mixed, values, preferred_element_type=F32)
    delta = jnp.sum(grad_probs * probs, axis=-1, keepdims=True)
    grad_scores = (probs * (grad_probs - delta)).astype(BF)
    grad_q = jnp.einsum("hqk,khd->qhd", grad_scores, keys, preferred_element_type=F32) * score_scale
    grad_k = jnp.einsum("hqk,qhd->khd", grad_scores, queries, preferred_element_type=F32) * score_scale
    grad_v = jnp.einsum("hqk,qhd->khd", probs_low, grad_mixed, preferred_element_type=F32)
    grad_q, grad_k, grad_v = [g.reshape(group, lw).astype(BF) for g in (grad_q, grad_k, grad_v)]
    grad_joined = jnp.concatenate([grad_q, grad_k, grad_v], axis=1)
    gw_proj = t_mm(mixed_all, atts).astype(BF).reshape(S, F, wr, width)
    gw_proj = lax.dynamic_index_in_dim(gw_proj, f, 1, keepdims=False)
    gw_qkv = t_mm(normed, grad_joined).astype(BF).reshape(S, F * wr, 3 * lw)
    part1 = mm_t(grad_joined, qkv)
    grad_g1 = jnp.sum(part1 * xhat1, axis=0)
    grad_b1 = jnp.sum(part1, axis=0)
    part1 = part1.astype(BF).reshape(F, rows, width)
    grad_first = net.scatter_sum([part1[k] for k in range(F)])
    grad_tokens = (grad_middle + norm_back(grad_first, g1, xhat1[:rows], scale1[:rows])).astype(BF)

    g_mlp = net.scatter_seq(jnp.concatenate([gw_down, gw_up], axis=2), BF)
    g_down = g_mlp[:, :width]
    g_up = g_mlp[:, width:].astype(BF).reshape(F, wr, lu)
    g_up = [p.reshape(wr, S, 1, ur) for p in net.exchange_pieces(g_up)]
    g_up = net.to_absolute(g_up, 2).astype(F32).reshape(wr, ff)
    gw_proj = gw_proj.reshape(S, wr, F, lw).transpose(0, 2, 1, 3).reshape(S, F * wr, lw)
    g_att = net.scatter_seq(jnp.concatenate([gw_qkv, gw_proj], axis=2), BF)
    g_proj = g_att[:, 3 * lw :].reshape(F, wr, lw).transpose(1, 0, 2).reshape(wr, width)
    g_qkv = g_att[:, : 3 * lw].astype(BF).reshape(F, wr, 3 * lw)
    g_qkv = [p.reshape(wr, 3, 1, lw) for p in net.exchange_pieces(g_qkv)]
    g_qkv = net.to_absolute(g_qkv, 2).astype(F32).reshape(wr, 3 * width)

    def spread(v):
        return lax.dynamic_update_slice_in_dim(jnp.zeros((width,), F32), v, f * lw, 0)

    full = [
        grad_g1,
        grad_b1,
        spread(jnp.sum(grad_q.astype(F32), axis=0)),
        spread(jnp.sum(grad_v.astype(F32), axis=0)),
        jnp.sum(att.astype(F32), axis=0),
        grad_g2,
        grad_b2,
        jnp.sum(upstream, axis=0),
    ]
    full = jnp.concatenate([v.reshape(S, F, wr) for v in full], axis=2)
    units = lax.dynamic_update_slice_in_dim(
        jnp.zeros((S, F, ur), F32), grad_ub.reshape(S, 1, ur), f, 1
    )
    sums = jnp.concatenate([full, units], axis=2)
    sums = scatter_small(net, sums)
    pick = lambda k: lax.dynamic_index_in_dim(sums, (f + k) % F, 0, keepdims=False)
    mine = pick(0)
    for k in range(1, F):
        mine = mine + net.shift(pick(k), k)
    v = [mine[i * wr : (i + 1) * wr] for i in range(8)]
    grad_up_bias = mine[8 * wr :]
    return (
        output,
        grad_tokens,
        v[0],
        v[1],
        g_qkv,
        v[2],
        v[3],
        g_proj,
        v[4],
        v[5],
        v[6],
        g_up,
        grad_up_bias,
        g_down,
        v[7],
    )


def scatter_small(net, x):
    cur = x
    bit = net.S // 2
    while bit:
        view = cur.reshape(2, bit, *x.shape[1:])
        my = jnp.where((net.s & bit) != 0, 1, 0)
        keep = lax.dynamic_index_in_dim(view, my, 0, keepdims=False)
        give = lax.dynamic_index_in_dim(view, 1 - my, 0, keepdims=False)
        cur = keep + net.swap(give, bit)
        bit //= 2
    return cur[0]


def solution(mesh):
    both = ("seq", "fsdp")
    mat, vec = P(both, None), P(both)
    sizes = (mesh.shape["seq"], mesh.shape["fsdp"])

    def body(*args):
        return on_device(sizes, *args)

    return jax.shard_map(
        body,
        mesh=mesh,
        in_specs=(mat, vec, vec, mat, vec, vec, mat, vec, vec, vec, mat, vec, mat, vec, mat, vec, vec),
        out_specs=(mat, mat, vec, vec, mat, vec, vec, mat, vec, vec, vec, mat, vec, mat, vec),
        check_vma=False,
    )
```
